32 devices in a mesh: px: 4 (over y, x), py: 8 (over z, core).
Axes of the slice: x: 2, y: 2, z: 4, core: 2. Of those that a mesh axis runs over, the one named last changes fastest.
Arguments:
- field: bfloat16 [32, 128, 128, 128], P(None, 'px', 'py'), may hold values from -6 to 6
- spec_fine: bfloat16 [2, 32, 32, 32, 32, 32], P(None, None, None, None, 'px', 'py'), may hold values from -18 to 18
- mix_fine: bfloat16 [32, 32], replicated, may hold values from -1 to 1
- bias_fine: float32 [32], replicated, may hold values from -3 to 3
- spec_coarse: bfloat16 [2, 32, 32, 32, 32, 32], P(None, None, None, None, 'px', 'py'), may hold values from -12 to 12
- mix_coarse: bfloat16 [32, 32], replicated, may hold values from -1 to 1
- bias_coarse: float32 [32], replicated, may hold values from -3 to 3
Outputs:
- output: bfloat16 [32, 128, 128, 128], P(None, 'px', 'py')
The draws below stay inside these ranges and needn't reach their ends.
All inputs are finite; a program needn't handle non-finite values.
Results may differ from the reference program's by a relative error of at most 0.0085.
Values may be sent and summed in bfloat16 or wider, within the bound.
A program may use at most 192 MiB of HBM per device.

```python
import math
import jax
import jax.numpy as jnp
from jax import lax

C = 32
N = 128
KX = 32
KY = 32
KZ = 32


def level_of(rng, shape, split, smallest, largest):
    gain = 1.0
    for position, shards_of in split:
        heights = jax.random.uniform(jax.random.fold_in(jax.random.fold_in(rng, 6), position), (shards_of,), jnp.float32, smallest / len(split), largest / len(split))
        gain = gain * jnp.repeat(jnp.exp(heights), shape[position] // shards_of).reshape((-1,) + (1,) * (len(shape) - 1 - position))
    return gain


def normal_values(rng, extent, spread, reach, cuts=(), kind=jnp.bfloat16):
    result = jax.random.normal(rng, extent, jnp.float32) * spread
    if len(cuts) > 0:
        result = level_of(rng, extent, cuts, -0.22, 0.18) * result
    return jnp.clip(result, min=-reach, max=reach).astype(kind)


def setup_inputs(seed: int = 0) -> dict:
    streams_of = jax.random.split(jax.random.key(seed), 8)
    return {
        "field": normal_values(streams_of[0], (C, N, N, N), 1.0, 6.0, ((1, 4), (2, 8))),
        "spec_fine": normal_values(streams_of[1], (2, C, C, KX, KY, KZ), 3.0, 18.0, ((4, 4), (5, 8))),
        "mix_fine": normal_values(streams_of[2], (C, C), C ** -0.5, 1.0),
        "bias_fine": normal_values(streams_of[3], (C,), 0.5, 3.0, (), jnp.float32),
        "spec_coarse": normal_values(streams_of[4], (2, C, C, KX, KY, KZ), 2.0, 12.0, ((4, 4), (5, 8))),
        "mix_coarse": normal_values(streams_of[5], (C, C), C ** -0.5, 1.0),
        "bias_coarse": normal_values(streams_of[6], (C,), 0.5, 3.0, (), jnp.float32),
    }


highest = lax.Precision.HIGHEST


def phases(cells, modes, offset):
    places = jnp.arange(cells, dtype=jnp.int32)
    frequency = jnp.arange(modes, dtype=jnp.int32) - offset
    windings = (places[:, None] * frequency[None, :]) % cells
    return windings.astype(jnp.float32) * (2.0 * math.pi / cells)


def forward_table(cells, modes, offset):
    angle = phases(cells, modes, offset)
    return jnp.stack([jnp.cos(angle), -jnp.sin(angle)]).astype(jnp.bfloat16)


def inverse_table(cells, modes, offset):
    angle = phases(cells, modes, offset)
    return jnp.transpose(jnp.stack([jnp.cos(angle), jnp.sin(angle)]), (0, 2, 1))


def depth_inverse(cells, modes):
    angle = phases(cells, modes, 0)
    factor = jnp.where(jnp.arange(modes) == 0, 1.0, 2.0).astype(jnp.float32) / float(cells * cells * cells)
    return jnp.transpose(jnp.stack([factor[None, :] * jnp.cos(angle), -factor[None, :] * jnp.sin(angle)]), (0, 2, 1))


def complex_dot(data, table, form):
    real = jnp.einsum(form, data[0], table[0], precision=highest) - jnp.einsum(form, data[1], table[1], precision=highest)
    imag = jnp.einsum(form, data[0], table[1], precision=highest) + jnp.einsum(form, data[1], table[0], precision=highest)
    return jnp.stack([real, imag])


def mix_modes(modes, spectral):
    weights = spectral.astype(jnp.float32)
    form = "ijmk,iojmk->ojmk"
    real = jnp.einsum(form, modes[0], weights[0], precision=highest) - jnp.einsum(form, modes[1], weights[1], precision=highest)
    imag = jnp.einsum(form, modes[0], weights[1], precision=highest) + jnp.einsum(form, modes[1], weights[0], precision=highest)
    return jnp.stack([real, imag])


def spectral_layer(field, spectral, mixing, offsets):
    channels, cells = field.shape[0], field.shape[1]
    row_block = 16 if cells % 16 == 0 else cells
    depth_table = forward_table(cells, KZ, 0).astype(jnp.float32)
    column_table = forward_table(cells, KY, KY // 2).astype(jnp.float32)
    row_table = forward_table(cells, KX, KX // 2).astype(jnp.float32)

    def gather_step(total, slab_index):
        slab = lax.dynamic_slice_in_dim(field, slab_index * row_block, row_block, 1).astype(jnp.float32)
        depth = jnp.einsum("cxyz,rzk->rcxyk", slab, depth_table, precision=highest)
        across = complex_dot(depth, column_table, "cxyk,ym->cxmk")
        part_table = lax.dynamic_slice_in_dim(row_table, slab_index * row_block, row_block, 1)
        return total + complex_dot(across, part_table, "cxmk,xj->cjmk"), None

    start_modes = jnp.zeros((2, channels, KX, KY, KZ), jnp.float32)
    modes, _ = lax.scan(gather_step, start_modes, jnp.arange(cells // row_block, dtype=jnp.int32))
    mixed = mix_modes(modes, spectral)
    row_inverse = inverse_table(cells, KX, KX // 2)
    column_inverse = inverse_table(cells, KY, KY // 2)
    depth_back = depth_inverse(cells, KZ)
    mixing_wide = mixing.astype(jnp.float32)

    def slab_out(slab_index):
        part_table = lax.dynamic_slice_in_dim(row_inverse, slab_index * row_block, row_block, 2)
        rows_back = complex_dot(mixed, part_table, "cjmk,jx->cxmk")
        columns_back = complex_dot(rows_back, column_inverse, "cxmk,my->cxyk")
        spectral_part = jnp.einsum("cxyk,kz->cxyz", columns_back[0], depth_back[0], precision=highest)
        spectral_part = spectral_part + jnp.einsum("cxyk,kz->cxyz", columns_back[1], depth_back[1], precision=highest)
        slab = lax.dynamic_slice_in_dim(field, slab_index * row_block, row_block, 1).astype(jnp.float32)
        pointwise = jnp.einsum("cxyz,co->oxyz", slab, mixing_wide, precision=highest)
        total = spectral_part + pointwise + offsets[:, None, None, None].astype(jnp.float32)
        return jax.nn.gelu(total).astype(jnp.bfloat16)

    blocks = lax.map(slab_out, jnp.arange(cells // row_block, dtype=jnp.int32))
    return jnp.transpose(blocks, (1, 0, 2, 3, 4)).reshape(channels, cells, cells, cells)


def reference(field, spec_fine, mix_fine, bias_fine, spec_coarse, mix_coarse, bias_coarse):
    upper = spectral_layer(field, spec_fine, mix_fine, bias_fine)
    channels, rows_x, rows_y, cells = upper.shape
    blocks = upper.astype(jnp.float32).reshape(channels, rows_x // 2, 2, rows_y // 2, 2, cells // 2, 2)
    pooled = blocks.mean(axis=(2, 4, 6)).astype(jnp.bfloat16)
    lower = spectral_layer(pooled, spec_coarse, mix_coarse, bias_coarse)
    merged = blocks + lower.astype(jnp.float32)[:, :, None, :, None, :, None]
    return merged.reshape(channels, rows_x, rows_y, cells).astype(jnp.bfloat16)
```

```python
import math

import jax
import jax.numpy as jnp
from jax import lax
from jax.sharding import PartitionSpec as P

narrow = jnp.bfloat16
wide = jnp.float32


def phases(cells, modes, offset):
    places = jnp.arange(cells, dtype=jnp.int32)
    frequency = jnp.arange(modes, dtype=jnp.int32) - offset
    windings = places[:, None] * frequency[None, :] % cells
    return windings.astype(wide) * (2.0 * math.pi / cells)


def turn_table(cells, modes, offset, sign):
    angle = phases(cells, modes, offset)
    cos = jnp.cos(angle).astype(narrow)
    sin = (sign * jnp.sin(angle)).astype(narrow)
    return jnp.stack([jnp.stack([cos, sin], -1), jnp.stack([-sin, cos], -1)])


def depth_forward(cells, modes):
    angle = phases(cells, modes, 0)
    return jnp.stack([jnp.cos(angle), -jnp.sin(angle)], 1).astype(narrow)


def depth_inverse(cells, modes):
    angle = phases(cells, modes, 0)
    factor = jnp.where(jnp.arange(modes) == 0, 1.0, 2.0).astype(wide) / float(cells * cells * cells)
    return jnp.stack([factor * jnp.cos(angle), -factor * jnp.sin(angle)]).astype(narrow)


def dot(form, left, right, kind=narrow):
    return jnp.einsum(form, left, right, preferred_element_type=wide).astype(kind)


def swap(value, axis):
    return lax.all_to_all(value, axis, split_axis=0, concat_axis=0)


def mix_modes(modes, spectral):
    mr = modes[:, 0][:, None]
    mi = modes[:, 1][:, None]
    wr = spectral[0].astype(wide)
    wi = spectral[1].astype(wide)
    real = (mr * wr - mi * wi).sum(0)
    imag = (mr * wi + mi * wr).sum(0)
    return jnp.stack([real, imag], 1)


def spectral_layer(field, spectral, mixing, offsets):
    np_, ng = lax.axis_size("px"), lax.axis_size("py")
    c, xl, yl, cells = field.shape
    _, _, _, kx, ml, kl = spectral.shape
    ky, kz = ml * np_, kl * ng
    cb = c // np_
    row = turn_table(cells, kx, kx // 2, -1.0).reshape(2, np_, xl, kx, 2)
    column = turn_table(cells, ky, ky // 2, -1.0).reshape(2, ng, yl, np_, ml, 2)
    depth = depth_forward(cells, kz)
    row_back = turn_table(cells, kx, kx // 2, 1.0).reshape(2, np_, xl, kx, 2)
    column_back = turn_table(cells, ky, ky // 2, 1.0).reshape(2, ng, yl, np_, ml, 2)
    depth_back = depth_inverse(cells, kz)

    d = dot("cxyz,zrk->crkxy", field, depth).reshape(np_, cb, 2, kz, xl, yl)
    d = swap(d, "px").reshape(np_, cb, 2, ng, kl, xl, yl)
    e = dot("pcrgkxy,rpxjs->gcskjy", d, row)
    e = swap(e, "py")
    f = dot("hcskjy,shyqmt->qctjmk", e, column)
    f = swap(f, "px").reshape(c, 2, kx, ml, kl)
    mixed = mix_modes(f.astype(wide), spectral).astype(narrow)
    b = swap(mixed.reshape(np_, cb, 2, kx, ml, kl), "px")
    b = dot("pcujmk,uhypmv->hcvkjy", b, column_back)
    b = swap(b, "py")
    b = dot("gcvkjy,vpxjw->pcwgkxy", b, row_back)
    b = swap(b, "px").reshape(c, 2, kz, xl, yl)
    total = jnp.einsum("cwkxy,wzk->cxyz", b, depth_back, preferred_element_type=wide)
    total = total + jnp.einsum("cxyz,co->oxyz", field, mixing, preferred_element_type=wide)
    return jax.nn.gelu(total + offsets[:, None, None, None]).astype(narrow)


def on_device(field, spec_fine, mix_fine, bias_fine, spec_coarse, mix_coarse, bias_coarse):
    upper = spectral_layer(field, spec_fine, mix_fine, bias_fine)
    channels, rows_x, rows_y, cells = upper.shape
    blocks = upper.astype(wide).reshape(channels, rows_x // 2, 2, rows_y // 2, 2, cells // 2, 2)
    pooled = blocks.mean(axis=(2, 4, 6)).astype(narrow)
    lower = spectral_layer(pooled, spec_coarse, mix_coarse, bias_coarse)
    merged = blocks + lower.astype(wide)[:, :, None, :, None, :, None]
    return merged.reshape(channels, rows_x, rows_y, cells).astype(narrow)


def solution(mesh):
    return jax.shard_map(
        on_device,
        mesh=mesh,
        in_specs=(
            P(None, "px", "py", None),
            P(None, None, None, None, "px", "py"),
            P(),
            P(),
            P(None, None, None, None, "px", "py"),
            P(),
            P(),
        ),
        out_specs=P(None, "px", "py", None),
        check_vma=False,
    )
```

```python
import math

import jax
import jax.numpy as jnp
from jax import lax
from jax.experimental import pallas as pl
from jax.experimental.pallas import tpu as pltpu
from jax.sharding import PartitionSpec as P

narrow = jnp.bfloat16
wide = jnp.float32


def phases(cells, modes, offset):
    places = jnp.arange(cells, dtype=jnp.int32)
    frequency = jnp.arange(modes, dtype=jnp.int32) - offset
    windings = places[:, None] * frequency[None, :] % cells
    return windings.astype(wide) * (2.0 * math.pi / cells)


def turn_table(cells, modes, offset, sign):
    angle = phases(cells, modes, offset)
    cos = jnp.cos(angle).astype(narrow)
    sin = (sign * jnp.sin(angle)).astype(narrow)
    return jnp.stack([jnp.stack([cos, sin], -1), jnp.stack([-sin, cos], -1)])


def depth_forward(cells, modes):
    angle = phases(cells, modes, 0)
    return jnp.stack([jnp.cos(angle), -jnp.sin(angle)], 1).astype(narrow)


def depth_inverse(cells, modes):
    angle = phases(cells, modes, 0)
    factor = jnp.where(jnp.arange(modes) == 0, 1.0, 2.0).astype(wide) / float(cells * cells * cells)
    return jnp.stack([factor * jnp.cos(angle), -factor * jnp.sin(angle)]).astype(narrow)


def dot(form, left, right, kind=narrow):
    return jnp.einsum(form, left, right, preferred_element_type=wide).astype(kind)


def swap(value, axis):
    return lax.all_to_all(value, axis, split_axis=0, concat_axis=0)


def mix_modes(modes, spectral):
    mr = modes[:, 0][:, None]
    mi = modes[:, 1][:, None]
    wr = spectral[0].astype(wide)
    wi = spectral[1].astype(wide)
    real = (mr * wr - mi * wi).sum(0)
    imag = (mr * wi + mi * wr).sum(0)
    return jnp.stack([real, imag], 1)


def spectral_coefficients(field, spectral):
    np_, ng = lax.axis_size("px"), lax.axis_size("py")
    c, xl, yl, cells = field.shape
    _, _, _, kx, ml, kl = spectral.shape
    ky, kz = ml * np_, kl * ng
    cb = c // np_
    row = turn_table(cells, kx, kx // 2, -1.0).reshape(2, np_, xl, kx, 2)
    column = turn_table(cells, ky, ky // 2, -1.0).reshape(2, ng, yl, np_, ml, 2)
    depth = depth_forward(cells, kz)
    row_back = turn_table(cells, kx, kx // 2, 1.0).reshape(2, np_, xl, kx, 2)
    column_back = turn_table(cells, ky, ky // 2, 1.0).reshape(2, ng, yl, np_, ml, 2)
    depth_back = depth_inverse(cells, kz)

    d = depth_lines(field.reshape(c, xl * yl, cells), depth.reshape(cells, 2 * kz).T)
    d = swap(d.reshape(np_, cb, 2 * kz, xl * yl), "px").reshape(np_, cb, 2, ng, kl, xl, yl)
    e = dot("pcrgkxy,rpxjs->gcskjy", d, row)
    e = swap(e, "py")
    f = dot("hcskjy,shyqmt->qctjmk", e, column)
    f = swap(f, "px").reshape(c, 2, kx, ml, kl)
    mixed = mix_modes(f.astype(wide), spectral).astype(narrow)
    b = swap(mixed.reshape(np_, cb, 2, kx, ml, kl), "px")
    b = dot("pcujmk,uhypmv->hcvkjy", b, column_back)
    b = swap(b, "py")
    b = dot("gcvkjy,vpxjw->pcwgkxy", b, row_back)
    b = swap(b.reshape(np_, cb, 2 * kz, xl * yl), "px").reshape(c, 2 * kz, xl * yl)
    return b, jnp.transpose(depth_back, (0, 2, 1)).reshape(2 * kz, cells)


def gelu(v):
    return 0.5 * v * (1.0 + jnp.tanh(math.sqrt(2.0 / math.pi) * (v + 0.044715 * v * v * v)))


def depth_kernel(table, lines, out):
    for i in range(lines.shape[0]):
        out[i] = lax.dot_general(
            table[...], lines[i], (((1,), (1,)), ((), ())), preferred_element_type=wide
        ).astype(narrow)


def depth_lines(lines, table):
    c, points, cells = lines.shape
    step = 4 if c % 4 == 0 else 1
    return pl.pallas_call(
        depth_kernel,
        out_shape=jax.ShapeDtypeStruct((c, table.shape[0], points), narrow),
        grid=(c // step,),
        in_specs=[
            pl.BlockSpec(table.shape, lambda i: (0, 0)),
            pl.BlockSpec((step, points, cells), lambda i: (i, 0, 0)),
        ],
        out_specs=pl.BlockSpec((step, table.shape[0], points), lambda i: (i, 0, 0)),
        name="depth_lines",
    )(table, lines)


def spread(mixing, rows):
    c = mixing.shape[0]
    full = mixing.T[:, None, :, None] * jnp.eye(rows, dtype=narrow)[None, :, None, :]
    return full.reshape(c * rows, c * rows)


def column_of(offsets, rows):
    return jnp.broadcast_to(offsets[:, None], (offsets.shape[0], rows)).reshape(-1, 1)


def back_along_depth(coefficients, table, sums):
    c, xs, yl, cells = sums.shape
    for o in range(c):
        part = lax.dot_general(
            coefficients[o], table[...], (((0,), (0,)), ((), ())), preferred_element_type=wide
        )
        sums[o] = part.reshape(xs, yl, cells)


def upper_kernel(field, coefficients, table, mixing, offsets, pairs, upper, pooled, sums, half):
    c, xs, yl, cells = field.shape
    back_along_depth(coefficients, table, sums)
    for x in range(xs):
        lines = field[:, x].reshape(c * yl, cells)
        total = jnp.dot(mixing[...], lines, preferred_element_type=wide)
        total = total + sums[:, x].reshape(c * yl, cells) + offsets[...]
        value = gelu(total).astype(narrow)
        upper[:, x] = value.reshape(c, yl, cells)
        part = jnp.dot(value, pairs[...], preferred_element_type=wide)
        if x % 2 == 0:
            half[...] = part
        else:
            half[...] = half[...] + part
            rows = c * yl // 2
            mean = half[pl.ds(0, rows, 2), :] + half[pl.ds(1, rows, 2), :]
            mean = (mean * 0.125)[:, : cells // 2]
            pooled[:, x // 2] = mean.reshape(c, yl // 2, cells // 2).astype(narrow)


def upper_call(field, coefficients, table, mixing, offsets):
    c, xl, yl, cells = field.shape
    xs = 128 // yl
    place = jnp.arange(cells)
    pairs = (place[:, None] // 2 == place[None, :]).astype(narrow)
    whole = lambda value: pl.BlockSpec(value.shape, lambda i: (0,) * value.ndim)
    mixing = spread(mixing, yl)
    offsets = column_of(offsets, yl)
    return pl.pallas_call(
        upper_kernel,
        out_shape=(
            jax.ShapeDtypeStruct(field.shape, narrow),
            jax.ShapeDtypeStruct((c, xl // 2, yl // 2, cells // 2), narrow),
        ),
        grid=(xl // xs,),
        in_specs=[
            pl.BlockSpec((c, xs, yl, cells), lambda i: (0, i, 0, 0)),
            pl.BlockSpec((c, table.shape[0], xs * yl), lambda i: (0, 0, i)),
            whole(table),
            whole(mixing),
            whole(offsets),
            whole(pairs),
        ],
        out_specs=(
            pl.BlockSpec((c, xs, yl, cells), lambda i: (0, i, 0, 0)),
            pl.BlockSpec((c, xs // 2, yl // 2, cells // 2), lambda i: (0, i, 0, 0)),
        ),
        scratch_shapes=[
            pltpu.VMEM((c, xs, yl, cells), wide),
            pltpu.VMEM((c * yl, cells), wide),
        ],
        compiler_params=pltpu.CompilerParams(vmem_limit_bytes=48 * 2**20),
        name="upper_call",
    )(field, coefficients, table, mixing, offsets, pairs)


def merge_kernel(upper, pooled, coefficients, table, mixing, offsets, twice, out, sums, lifted):
    c, xs, yl, cells = pooled.shape
    step = pl.program_id(0)

    @pl.when(step == 0)
    def _():
        back_along_depth(coefficients, table, sums)

    for x in range(xs):
        lines = pooled[:, x].astype(wide).reshape(c * yl, cells).astype(narrow)
        total = jnp.dot(mixing[...], lines, preferred_element_type=wide)
        total = total + sums[:, step * xs + x].reshape(c * yl, cells) + offsets[...]
        value = gelu(total).astype(narrow)
        wider = jnp.dot(value, twice[...], preferred_element_type=wide)
        lifted[pl.ds(0, c * yl, 2), :] = wider
        lifted[pl.ds(1, c * yl, 2), :] = wider
        for side in range(2):
            fine = upper[:, 2 * x + side].astype(wide).reshape(2 * c * yl, 2 * cells)
            out[:, 2 * x + side] = (fine + lifted[...]).astype(narrow).reshape(c, 2 * yl, 2 * cells)


def merge_call(upper, pooled, coefficients, table, mixing, offsets):
    c, xl, yl, cells = pooled.shape
    xs = 2
    twice = (jnp.arange(cells)[:, None] == jnp.arange(2 * cells)[None, :] // 2).astype(narrow)
    whole = lambda value: pl.BlockSpec(value.shape, lambda i: (0,) * value.ndim)
    mixing = spread(mixing, yl)
    offsets = column_of(offsets, yl)
    fine = pl.BlockSpec((c, 2 * xs, 2 * yl, 2 * cells), lambda i: (0, i, 0, 0))
    return pl.pallas_call(
        merge_kernel,
        out_shape=jax.ShapeDtypeStruct(upper.shape, narrow),
        grid=(xl // xs,),
        in_specs=[
            fine,
            pl.BlockSpec((c, xs, yl, cells), lambda i: (0, i, 0, 0)),
            whole(coefficients),
            whole(table),
            whole(mixing),
            whole(offsets),
            whole(twice),
        ],
        out_specs=fine,
        scratch_shapes=[
            pltpu.VMEM((c, xl, yl, cells), wide),
            pltpu.VMEM((2 * c * yl, 2 * cells), wide),
        ],
        compiler_params=pltpu.CompilerParams(vmem_limit_bytes=48 * 2**20),
        name="merge_call",
    )(upper, pooled, coefficients, table, mixing, offsets, twice)


def plain_layer(field, coefficients, table, mixing, offsets):
    c, xl, yl, cells = field.shape
    total = jnp.einsum("cnp,nz->cpz", coefficients, table, preferred_element_type=wide)
    total = total.reshape(field.shape)
    total = total + jnp.einsum("cxyz,co->oxyz", field, mixing, preferred_element_type=wide)
    return gelu(total + offsets[:, None, None, None]).astype(narrow)


def plain_pool(upper):
    c, xl, yl, cells = upper.shape
    blocks = upper.astype(wide).reshape(c, xl // 2, 2, yl // 2, 2, cells // 2, 2)
    return blocks.mean(axis=(2, 4, 6)).astype(narrow)


def plain_merge(upper, lower):
    c, xl, yl, cells = upper.shape
    blocks = upper.astype(wide).reshape(c, xl // 2, 2, yl // 2, 2, cells // 2, 2)
    merged = blocks + lower.astype(wide)[:, :, None, :, None, :, None]
    return merged.reshape(upper.shape).astype(narrow)


def on_device(field, spec_fine, mix_fine, bias_fine, spec_coarse, mix_coarse, bias_coarse):
    c, xl, yl, cells = field.shape
    tiled = yl % 16 == 0 and 128 % yl == 0 and (xl * yl) % 128 == 0 and xl % 4 == 0
    found, table = spectral_coefficients(field, spec_fine)
    if tiled:
        upper, pooled = upper_call(field, found, table, mix_fine, bias_fine)
    else:
        upper = plain_layer(field, found, table, mix_fine, bias_fine)
        pooled = plain_pool(upper)
    found, table = spectral_coefficients(pooled, spec_coarse)
    if tiled:
        return merge_call(upper, pooled, found, table, mix_coarse, bias_coarse)
    return plain_merge(upper, plain_layer(pooled, found, table, mix_coarse, bias_coarse))


def solution(mesh):
    return jax.shard_map(
        on_device,
        mesh=mesh,
        in_specs=(
            P(None, "px", "py", None),
            P(None, None, None, None, "px", "py"),
            P(),
            P(),
            P(None, None, None, None, "px", "py"),
            P(),
            P(),
        ),
        out_specs=P(None, "px", "py", None),
        check_vma=False,
    )
```

```python
import functools
import math

import jax
import jax.numpy as jnp
from jax import lax
from jax.experimental import pallas as pl
from jax.experimental.pallas import tpu as pltpu
from jax.sharding import PartitionSpec as P

narrow = jnp.bfloat16
wide = jnp.float32


def phases(cells, modes, offset):
    places = jnp.arange(cells, dtype=jnp.int32)
    frequency = jnp.arange(modes, dtype=jnp.int32) - offset
    windings = places[:, None] * frequency[None, :] % cells
    return windings.astype(wide) * (2.0 * math.pi / cells)


def turn_table(cells, modes, offset, sign):
    angle = phases(cells, modes, offset)
    cos = jnp.cos(angle).astype(narrow)
    sin = (sign * jnp.sin(angle)).astype(narrow)
    return jnp.stack([jnp.stack([cos, sin], -1), jnp.stack([-sin, cos], -1)])


def depth_forward(cells, modes):
    angle = phases(cells, modes, 0)
    return jnp.stack([jnp.cos(angle), -jnp.sin(angle)], 1).astype(narrow)


def depth_inverse(cells, modes):
    angle = phases(cells, modes, 0)
    factor = jnp.where(jnp.arange(modes) == 0, 1.0, 2.0).astype(wide) / float(cells * cells * cells)
    return jnp.stack([factor * jnp.cos(angle), -factor * jnp.sin(angle)]).astype(narrow)


def dot(form, left, right, kind=narrow):
    return jnp.einsum(form, left, right, preferred_element_type=wide).astype(kind)


def swap(value, axis):
    return lax.all_to_all(value, axis, split_axis=0, concat_axis=0)


def mix_modes(modes, spectral):
    mr = modes[:, 0][:, None]
    mi = modes[:, 1][:, None]
    wr = spectral[0].astype(wide)
    wi = spectral[1].astype(wide)
    real = (mr * wr - mi * wi).sum(0)
    imag = (mr * wi + mi * wr).sum(0)
    return jnp.stack([real, imag], 1)


def spectral_coefficients(field, spectral):
    np_, ng = lax.axis_size("px"), lax.axis_size("py")
    c, xl, yl, cells = field.shape
    _, _, _, kx, ml, kl = spectral.shape
    ky, kz = ml * np_, kl * ng
    cb = c // np_
    row = turn_table(cells, kx, kx // 2, -1.0).reshape(2, np_, xl, kx, 2)
    column = turn_table(cells, ky, ky // 2, -1.0).reshape(2, ng, yl, np_, ml, 2)
    depth = depth_forward(cells, kz)
    row_back = turn_table(cells, kx, kx // 2, 1.0).reshape(2, np_, xl, kx, 2)
    column_back = turn_table(cells, ky, ky // 2, 1.0).reshape(2, ng, yl, np_, ml, 2)
    depth_back = depth_inverse(cells, kz)

    d = depth_lines(field.reshape(c, xl * yl, cells), depth.reshape(cells, 2 * kz).T)
    d = swap(d.reshape(np_, cb, 2 * kz, xl * yl), "px").reshape(np_, cb, 2, ng, kl, xl, yl)
    e = dot("pcrgkxy,rpxjs->gcskjy", d, row)
    e = swap(e, "py")
    f = dot("hcskjy,shyqmt->qctjmk", e, column)
    f = swap(f, "px").reshape(c, 2, kx, ml, kl)
    mixed = mix_modes(f.astype(wide), spectral).astype(narrow)
    b = swap(mixed.reshape(np_, cb, 2, kx, ml, kl), "px")
    b = dot("pcujmk,uhypmv->hcvkjy", b, column_back)
    b = swap(b, "py")
    b = dot("gcvkjy,vpxjw->pcwgkxy", b, row_back)
    b = swap(b.reshape(np_, cb, 2 * kz, xl * yl), "px").reshape(c, 2 * kz, xl * yl)
    return b, jnp.transpose(depth_back, (0, 2, 1)).reshape(2 * kz, cells)


def row_tables(table, quota):
    parts, blocks, xl, kx, _ = table.shape
    eye = jnp.eye(quota, dtype=narrow)
    full = jnp.einsum("rpxjs,yv->pryxsvj", table, eye)
    return full.reshape(blocks, parts, quota * xl, parts * quota * kx)


def row_back_tables(table, quota):
    parts, blocks, xl, kx, _ = table.shape
    eye = jnp.eye(quota, dtype=narrow)
    full = jnp.einsum("vpxjw,yu->vpyjwux", table, eye)
    return full.reshape(parts, blocks, quota * kx, parts * quota * xl)


def rows_kernel(d, table, out):
    blocks, cs, both, _ = d.shape
    kz = both // 2
    groups, _, _, kl, _ = out.shape
    take, give = table.shape[2], table.shape[3] // 2
    for t in range(d.shape[3] // take):
        total = 0.0
        for p in range(blocks):
            for r in range(2):
                part = d[p, :, r * kz : (r + 1) * kz, t * take : (t + 1) * take]
                part = part.reshape(cs * kz, take)
                total = total + jnp.dot(part, table[p, r], preferred_element_type=wide)
        for s in range(2):
            for c in range(cs):
                for g in range(groups):
                    rows = total[c * kz + g * kl : c * kz + (g + 1) * kl, s * give : (s + 1) * give]
                    out[g, c, s, :, t * give : (t + 1) * give] = rows.astype(narrow)


def rows_call(d, table, groups):
    blocks, cb, both, points = d.shape
    take, give = table.shape[2], table.shape[3] // 2
    width = points // take * give
    kl = both // 2 // groups
    cs = 4 if cb % 4 == 0 else 1
    return pl.pallas_call(
        rows_kernel,
        out_shape=jax.ShapeDtypeStruct((groups, cb, 2, kl, width), narrow),
        grid=(cb // cs,),
        in_specs=[
            pl.BlockSpec((blocks, cs, both, points), lambda i: (0, i, 0, 0)),
            pl.BlockSpec(table.shape, lambda i: (0, 0, 0, 0)),
        ],
        out_specs=pl.BlockSpec((groups, cs, 2, kl, width), lambda i: (0, i, 0, 0, 0)),
        name="rows_call",
    )(d, table)


def rows_back_kernel(b, table, out, lines):
    groups, cs, _, kl, width = b.shape
    blocks = out.shape[0]
    kz = groups * kl
    take, give = table.shape[2], table.shape[3] // 2
    for v in range(2):
        for c in range(cs):
            for g in range(groups):
                at = c * kz + g * kl
                lines[v, at : at + kl, :] = b[g, c, v].astype(wide)
    for t in range(width // take):
        parts = [lines[v, :, t * take : (t + 1) * take].astype(narrow) for v in range(2)]
        for p in range(blocks):
            total = jnp.dot(parts[0], table[0, p], preferred_element_type=wide)
            total = total + jnp.dot(parts[1], table[1, p], preferred_element_type=wide)
            for w in range(2):
                rows = total[:, w * give : (w + 1) * give].reshape(cs, kz, give)
                out[p, :, w * kz : (w + 1) * kz, t * give : (t + 1) * give] = rows.astype(narrow)


def rows_back_call(b, table):
    groups, cb, _, kl, width = b.shape
    blocks = table.shape[1]
    take, give = table.shape[2], table.shape[3] // 2
    points = width // take * give
    kz = groups * kl
    cs = 4 if cb % 4 == 0 else 1
    return pl.pallas_call(
        rows_back_kernel,
        out_shape=jax.ShapeDtypeStruct((blocks, cb, 2 * kz, points), narrow),
        grid=(cb // cs,),
        in_specs=[
            pl.BlockSpec((groups, cs, 2, kl, width), lambda i: (0, i, 0, 0, 0)),
            pl.BlockSpec(table.shape, lambda i: (0, 0, 0, 0)),
        ],
        out_specs=pl.BlockSpec((blocks, cs, 2 * kz, points), lambda i: (0, i, 0, 0)),
        scratch_shapes=[pltpu.VMEM((2, cs * kz, width), wide)],
        name="rows_back_call",
    )(b, table)


def tiled_coefficients(field, spectral):
    np_, ng = lax.axis_size("px"), lax.axis_size("py")
    c, xl, yl, cells = field.shape
    _, _, _, kx, ml, kl = spectral.shape
    ky, kz = ml * np_, kl * ng
    cb = c // np_
    quota = min(yl, 128 // xl)
    row = turn_table(cells, kx, kx // 2, -1.0).reshape(2, np_, xl, kx, 2)
    column = turn_table(cells, ky, ky // 2, -1.0).reshape(2, ng, yl, np_, ml, 2)
    depth = depth_forward(cells, kz)
    row_back = turn_table(cells, kx, kx // 2, 1.0).reshape(2, np_, xl, kx, 2)
    column_back = turn_table(cells, ky, ky // 2, 1.0).reshape(2, ng, yl, np_, ml, 2)
    depth_back = depth_inverse(cells, kz)

    d = depth_lines(field.reshape(c, xl * yl, cells), depth.reshape(cells, 2 * kz).T, yl)
    d = swap(d.reshape(np_, cb, 2 * kz, xl * yl), "px")
    e = swap(rows_call(d, row_tables(row, quota), ng), "py")
    e = e.reshape(ng, cb, 2, kl, yl, kx)
    f = dot("hcskyj,shyqmt->qctmkj", e, column)
    f = swap(f, "px").reshape(c, 2, ml, kl, kx)
    mixed = mix_modes(jnp.transpose(f, (0, 1, 4, 2, 3)).astype(wide), spectral).astype(narrow)
    mixed = jnp.transpose(mixed, (0, 1, 3, 4, 2))
    b = swap(mixed.reshape(np_, cb, 2, ml, kl, kx), "px")
    b = dot("pcumkj,uhypmv->hcvkyj", b, column_back)
    b = swap(b.reshape(ng, cb, 2, kl, yl * kx), "py")
    b = swap(rows_back_call(b, row_back_tables(row_back, quota)), "px")
    b = b.reshape(c, 2 * kz, xl * yl)
    return b, jnp.transpose(depth_back, (0, 2, 1)).reshape(2 * kz, cells)


def gelu(v):
    return 0.5 * v * (1.0 + jnp.tanh(math.sqrt(2.0 / math.pi) * (v + 0.044715 * v * v * v)))


def depth_kernel(yl, table, lines, out, held):
    points = lines.shape[1]
    for i in range(lines.shape[0]):
        cells = lines[i]
        if yl:
            held[...] = cells.astype(wide)
            cells = [held[pl.ds(y, points // yl, yl), :] for y in range(yl)]
            cells = jnp.concatenate(cells, 0).astype(narrow)
        out[i] = lax.dot_general(
            table[...], cells, (((1,), (1,)), ((), ())), preferred_element_type=wide
        ).astype(narrow)


def depth_lines(lines, table, yl=0):
    c, points, cells = lines.shape
    step = 4 if c % 4 == 0 else 1
    return pl.pallas_call(
        functools.partial(depth_kernel, yl),
        out_shape=jax.ShapeDtypeStruct((c, table.shape[0], points), narrow),
        grid=(c // step,),
        in_specs=[
            pl.BlockSpec(table.shape, lambda i: (0, 0)),
            pl.BlockSpec((step, points, cells), lambda i: (i, 0, 0)),
        ],
        out_specs=pl.BlockSpec((step, table.shape[0], points), lambda i: (i, 0, 0)),
        scratch_shapes=[pltpu.VMEM((points, cells), wide)],
        name="depth_lines",
    )(table, lines)


def spread(mixing, rows):
    c = mixing.shape[0]
    place = jnp.arange(c * rows)
    pick = (place[:, None] // rows == jnp.arange(c)[None, :]).astype(narrow)
    full = dot("on,np->op", pick, dot("nc,pc->np", mixing.T, pick), wide)
    return jnp.where(place[:, None] % rows == place[None, :] % rows, full, 0.0).astype(narrow)


def column_of(offsets, rows):
    return jnp.broadcast_to(offsets[:, None], (offsets.shape[0], rows)).reshape(-1, 1)


def back_along_depth(coefficients, table, sums, xl, yl):
    for o in range(sums.shape[0]):
        part = lax.dot_general(
            coefficients[o], table[...], (((0,), (0,)), ((), ())), preferred_element_type=wide
        )
        for y in range(yl):
            sums[o, pl.ds(y, xl, yl), :] = part[y * xl : (y + 1) * xl]


def upper_kernel(field, coefficients, table, mixing, offsets, pairs, upper, pooled, sums, half):
    c, xs, yl, cells = field.shape
    step = pl.program_id(0)

    @pl.when(step == 0)
    def _():
        back_along_depth(coefficients, table, sums, sums.shape[1] // yl, yl)

    for x in range(xs):
        lines = field[:, x].reshape(c * yl, cells)
        total = jnp.dot(mixing[...], lines, preferred_element_type=wide)
        total = total + sums[:, pl.ds(pl.multiple_of((step * xs + x) * yl, 8), yl), :].reshape(c * yl, cells) + offsets[...]
        value = gelu(total).astype(narrow)
        upper[:, x] = value.reshape(c, yl, cells)
        part = jnp.dot(value, pairs[...], preferred_element_type=wide)
        if x % 2 == 0:
            half[...] = part
        else:
            half[...] = half[...] + part
            rows = c * yl // 2
            mean = half[pl.ds(0, rows, 2), :] + half[pl.ds(1, rows, 2), :]
            mean = (mean * 0.125)[:, : cells // 2]
            pooled[:, x // 2] = mean.reshape(c, yl // 2, cells // 2).astype(narrow)


def upper_call(field, coefficients, table, mixing, offsets):
    c, xl, yl, cells = field.shape
    xs = 4
    place = jnp.arange(cells)
    pairs = (place[:, None] // 2 == place[None, :]).astype(narrow)
    whole = lambda value: pl.BlockSpec(value.shape, lambda i: (0,) * value.ndim)
    mixing = spread(mixing, yl)
    offsets = column_of(offsets, yl)
    return pl.pallas_call(
        upper_kernel,
        out_shape=(
            jax.ShapeDtypeStruct(field.shape, narrow),
            jax.ShapeDtypeStruct((c, xl // 2, yl // 2, cells // 2), narrow),
        ),
        grid=(xl // xs,),
        in_specs=[
            pl.BlockSpec((c, xs, yl, cells), lambda i: (0, i, 0, 0)),
            whole(coefficients),
            whole(table),
            whole(mixing),
            whole(offsets),
            whole(pairs),
        ],
        out_specs=(
            pl.BlockSpec((c, xs, yl, cells), lambda i: (0, i, 0, 0)),
            pl.BlockSpec((c, xs // 2, yl // 2, cells // 2), lambda i: (0, i, 0, 0)),
        ),
        scratch_shapes=[
            pltpu.VMEM((c, xl * yl, cells), wide),
            pltpu.VMEM((c * yl, cells), wide),
        ],
        compiler_params=pltpu.CompilerParams(vmem_limit_bytes=48 * 2**20),
        name="upper_call",
    )(field, coefficients, table, mixing, offsets, pairs)


def merge_kernel(upper, pooled, coefficients, table, mixing, offsets, twice, out, sums, lifted):
    c, xs, yl, cells = pooled.shape
    step = pl.program_id(0)

    @pl.when(step == 0)
    def _():
        back_along_depth(coefficients, table, sums, sums.shape[1] // yl, yl)

    for x in range(xs):
        lines = pooled[:, x].astype(wide).reshape(c * yl, cells).astype(narrow)
        total = jnp.dot(mixing[...], lines, preferred_element_type=wide)
        total = total + sums[:, pl.ds(pl.multiple_of((step * xs + x) * yl, 8), yl), :].reshape(c * yl, cells) + offsets[...]
        value = gelu(total).astype(narrow)
        wider = jnp.dot(value, twice[...], preferred_element_type=wide)
        lifted[pl.ds(0, c * yl, 2), :] = wider
        lifted[pl.ds(1, c * yl, 2), :] = wider
        for side in range(2):
            fine = upper[:, 2 * x + side].astype(wide).reshape(2 * c * yl, 2 * cells)
            out[:, 2 * x + side] = (fine + lifted[...]).astype(narrow).reshape(c, 2 * yl, 2 * cells)


def merge_call(upper, pooled, coefficients, table, mixing, offsets):
    c, xl, yl, cells = pooled.shape
    xs = 2
    twice = (jnp.arange(cells)[:, None] == jnp.arange(2 * cells)[None, :] // 2).astype(narrow)
    whole = lambda value: pl.BlockSpec(value.shape, lambda i: (0,) * value.ndim)
    mixing = spread(mixing, yl)
    offsets = column_of(offsets, yl)
    fine = pl.BlockSpec((c, 2 * xs, 2 * yl, 2 * cells), lambda i: (0, i, 0, 0))
    return pl.pallas_call(
        merge_kernel,
        out_shape=jax.ShapeDtypeStruct(upper.shape, narrow),
        grid=(xl // xs,),
        in_specs=[
            fine,
            pl.BlockSpec((c, xs, yl, cells), lambda i: (0, i, 0, 0)),
            whole(coefficients),
            whole(table),
            whole(mixing),
            whole(offsets),
            whole(twice),
        ],
        out_specs=fine,
        scratch_shapes=[
            pltpu.VMEM((c, xl * yl, cells), wide),
            pltpu.VMEM((2 * c * yl, 2 * cells), wide),
        ],
        compiler_params=pltpu.CompilerParams(vmem_limit_bytes=48 * 2**20),
        name="merge_call",
    )(upper, pooled, coefficients, table, mixing, offsets, twice)


def plain_layer(field, coefficients, table, mixing, offsets):
    c, xl, yl, cells = field.shape
    total = jnp.einsum("cnp,nz->cpz", coefficients, table, preferred_element_type=wide)
    total = total.reshape(field.shape)
    total = total + jnp.einsum("cxyz,co->oxyz", field, mixing, preferred_element_type=wide)
    return gelu(total + offsets[:, None, None, None]).astype(narrow)


def plain_pool(upper):
    c, xl, yl, cells = upper.shape
    blocks = upper.astype(wide).reshape(c, xl // 2, 2, yl // 2, 2, cells // 2, 2)
    return blocks.mean(axis=(2, 4, 6)).astype(narrow)


def plain_merge(upper, lower):
    c, xl, yl, cells = upper.shape
    blocks = upper.astype(wide).reshape(c, xl // 2, 2, yl // 2, 2, cells // 2, 2)
    merged = blocks + lower.astype(wide)[:, :, None, :, None, :, None]
    return merged.reshape(upper.shape).astype(narrow)


def on_device(field, spec_fine, mix_fine, bias_fine, spec_coarse, mix_coarse, bias_coarse):
    c, xl, yl, cells = field.shape
    tiled = yl % 16 == 0 and 128 % yl == 0 and (xl * yl) % 128 == 0 and xl % 4 == 0 and 128 % xl == 0
    find = tiled_coefficients if tiled else spectral_coefficients
    found, table = find(field, spec_fine)
    if tiled:
        upper, pooled = upper_call(field, found, table, mix_fine, bias_fine)
    else:
        upper = plain_layer(field, found, table, mix_fine, bias_fine)
        pooled = plain_pool(upper)
    found, table = find(pooled, spec_coarse)
    if tiled:
        return merge_call(upper, pooled, found, table, mix_coarse, bias_coarse)
    return plain_merge(upper, plain_layer(pooled, found, table, mix_coarse, bias_coarse))


def solution(mesh):
    return jax.shard_map(
        on_device,
        mesh=mesh,
        in_specs=(
            P(None, "px", "py", None),
            P(None, None, None, None, "px", "py"),
            P(),
            P(),
            P(None, None, None, None, "px", "py"),
            P(),
            P(),
        ),
        out_specs=P(None, "px", "py", None),
        check_vma=False,
    )
```

```python
import functools
import math

import jax
import jax.numpy as jnp
from jax import lax
from jax.experimental import pallas as pl
from jax.experimental.pallas import tpu as pltpu
from jax.sharding import PartitionSpec as P

narrow = jnp.bfloat16
wide = jnp.float32


def phases(cells, modes, offset):
    places = jnp.arange(cells, dtype=jnp.int32)
    frequency = jnp.arange(modes, dtype=jnp.int32) - offset
    windings = places[:, None] * frequency[None, :] % cells
    return windings.astype(wide) * (2.0 * math.pi / cells)


def turn_table(cells, modes, offset, sign):
    angle = phases(cells, modes, offset)
    cos = jnp.cos(angle).astype(narrow)
    sin = (sign * jnp.sin(angle)).astype(narrow)
    return jnp.stack([jnp.stack([cos, sin], -1), jnp.stack([-sin, cos], -1)])


def depth_forward(cells, modes):
    angle = phases(cells, modes, 0)
    return jnp.stack([jnp.cos(angle), -jnp.sin(angle)], 1).astype(narrow)


def depth_inverse(cells, modes):
    angle = phases(cells, modes, 0)
    factor = jnp.where(jnp.arange(modes) == 0, 1.0, 2.0).astype(wide) / float(cells * cells * cells)
    return jnp.stack([factor * jnp.cos(angle), -factor * jnp.sin(angle)]).astype(narrow)


def dot(form, left, right, kind=narrow):
    return jnp.einsum(form, left, right, preferred_element_type=wide).astype(kind)


def swap(value, axis):
    return lax.all_to_all(value, axis, split_axis=0, concat_axis=0)


def mix_modes(modes, spectral):
    mr = modes[:, 0][:, None]
    mi = modes[:, 1][:, None]
    wr = spectral[0].astype(wide)
    wi = spectral[1].astype(wide)
    real = (mr * wr - mi * wi).sum(0)
    imag = (mr * wi + mi * wr).sum(0)
    return jnp.stack([real, imag], 1)


def spectral_coefficients(field, spectral):
    np_, ng = lax.axis_size("px"), lax.axis_size("py")
    c, xl, yl, cells = field.shape
    _, _, _, kx, ml, kl = spectral.shape
    ky, kz = ml * np_, kl * ng
    cb = c // np_
    row = turn_table(cells, kx, kx // 2, -1.0).reshape(2, np_, xl, kx, 2)
    column = turn_table(cells, ky, ky // 2, -1.0).reshape(2, ng, yl, np_, ml, 2)
    depth = depth_forward(cells, kz)
    row_back = turn_table(cells, kx, kx // 2, 1.0).reshape(2, np_, xl, kx, 2)
    column_back = turn_table(cells, ky, ky // 2, 1.0).reshape(2, ng, yl, np_, ml, 2)
    depth_back = depth_inverse(cells, kz)

    d = depth_lines(field.reshape(c, xl * yl, cells), depth.reshape(cells, 2 * kz).T)
    d = swap(d.reshape(np_, cb, 2 * kz, xl * yl), "px").reshape(np_, cb, 2, ng, kl, xl, yl)
    e = dot("pcrgkxy,rpxjs->gcskjy", d, row)
    e = swap(e, "py")
    f = dot("hcskjy,shyqmt->qctjmk", e, column)
    f = swap(f, "px").reshape(c, 2, kx, ml, kl)
    mixed = mix_modes(f.astype(wide), spectral).astype(narrow)
    b = swap(mixed.reshape(np_, cb, 2, kx, ml, kl), "px")
    b = dot("pcujmk,uhypmv->hcvkjy", b, column_back)
    b = swap(b, "py")
    b = dot("gcvkjy,vpxjw->pcwgkxy", b, row_back)
    b = swap(b.reshape(np_, cb, 2 * kz, xl * yl), "px").reshape(c, 2 * kz, xl * yl)
    return b, jnp.transpose(depth_back, (0, 2, 1)).reshape(2 * kz, cells)


def line_tables(shape, split, cell_at, cells, offset, sign):
    near, far, quota = split
    iota = lambda axis: lax.broadcasted_iota(jnp.int32, shape, axis)
    row, column = iota(2), iota(3)
    cell, mode = (row % near, column % far) if cell_at == 0 else (column % far, row % near)
    blocks, part = (iota(0), iota(1)) if cell_at == 0 else (iota(1), iota(0))
    side = near if cell_at == 0 else far
    other = column // (quota * far)
    angle = ((blocks * side + cell) * (mode - offset) % cells).astype(wide) * (2.0 * math.pi / cells)
    sin = jnp.where(other == 1, sign, -sign) * jnp.sin(angle)
    value = jnp.where(part == other, jnp.cos(angle), sin)
    same = row // near == column // far % quota
    return jnp.where(same, value, 0.0).astype(narrow)


def rows_kernel(d, table, out):
    blocks, cs, both, _ = d.shape
    kz = both // 2
    groups, _, _, kl, _ = out.shape
    take, give = table.shape[2], table.shape[3] // 2
    for t in range(d.shape[3] // take):
        total = 0.0
        for p in range(blocks):
            for r in range(2):
                part = d[p, :, r * kz : (r + 1) * kz, t * take : (t + 1) * take]
                part = part.reshape(cs * kz, take)
                total = total + jnp.dot(part, table[p, r], preferred_element_type=wide)
        for s in range(2):
            for c in range(cs):
                for g in range(groups):
                    rows = total[c * kz + g * kl : c * kz + (g + 1) * kl, s * give : (s + 1) * give]
                    out[g, c, s, :, t * give : (t + 1) * give] = rows.astype(narrow)


def rows_call(d, table, groups):
    blocks, cb, both, points = d.shape
    take, give = table.shape[2], table.shape[3] // 2
    width = points // take * give
    kl = both // 2 // groups
    cs = 4 if cb % 4 == 0 else 1
    return pl.pallas_call(
        rows_kernel,
        out_shape=jax.ShapeDtypeStruct((groups, cb, 2, kl, width), narrow),
        grid=(cb // cs,),
        in_specs=[
            pl.BlockSpec((blocks, cs, both, points), lambda i: (0, i, 0, 0)),
            pl.BlockSpec(table.shape, lambda i: (0, 0, 0, 0)),
        ],
        out_specs=pl.BlockSpec((groups, cs, 2, kl, width), lambda i: (0, i, 0, 0, 0)),
        name="rows_call",
    )(d, table)


def rows_back_kernel(b, table, out, lines):
    groups, cs, _, kl, width = b.shape
    blocks = out.shape[0]
    kz = groups * kl
    take, give = table.shape[2], table.shape[3] // 2
    for v in range(2):
        for c in range(cs):
            for g in range(groups):
                at = c * kz + g * kl
                lines[v, at : at + kl, :] = b[g, c, v].astype(wide)
    for t in range(width // take):
        parts = [lines[v, :, t * take : (t + 1) * take].astype(narrow) for v in range(2)]
        for p in range(blocks):
            total = jnp.dot(parts[0], table[0, p], preferred_element_type=wide)
            total = total + jnp.dot(parts[1], table[1, p], preferred_element_type=wide)
            for w in range(2):
                rows = total[:, w * give : (w + 1) * give].reshape(cs, kz, give)
                out[p, :, w * kz : (w + 1) * kz, t * give : (t + 1) * give] = rows.astype(narrow)


def rows_back_call(b, table):
    groups, cb, _, kl, width = b.shape
    blocks = table.shape[1]
    take, give = table.shape[2], table.shape[3] // 2
    points = width // take * give
    kz = groups * kl
    cs = 4 if cb % 4 == 0 else 1
    return pl.pallas_call(
        rows_back_kernel,
        out_shape=jax.ShapeDtypeStruct((blocks, cb, 2 * kz, points), narrow),
        grid=(cb // cs,),
        in_specs=[
            pl.BlockSpec((groups, cs, 2, kl, width), lambda i: (0, i, 0, 0, 0)),
            pl.BlockSpec(table.shape, lambda i: (0, 0, 0, 0)),
        ],
        out_specs=pl.BlockSpec((blocks, cs, 2 * kz, points), lambda i: (0, i, 0, 0)),
        scratch_shapes=[pltpu.VMEM((2, cs * kz, width), wide)],
        name="rows_back_call",
    )(b, table)


def tiled_coefficients(field, spectral):
    np_, ng = lax.axis_size("px"), lax.axis_size("py")
    c, xl, yl, cells = field.shape
    _, _, _, kx, ml, kl = spectral.shape
    ky, kz = ml * np_, kl * ng
    cb = c // np_
    quota = min(yl, 128 // xl)
    row = line_tables(
        (np_, 2, quota * xl, 2 * quota * kx), (xl, kx, quota), 0, cells, kx // 2, -1.0
    )
    column = turn_table(cells, ky, ky // 2, -1.0).reshape(2, ng, yl, np_, ml, 2)
    depth = depth_forward(cells, kz)
    row_back = line_tables(
        (2, np_, quota * kx, 2 * quota * xl), (kx, xl, quota), 1, cells, kx // 2, 1.0
    )
    column_back = turn_table(cells, ky, ky // 2, 1.0).reshape(2, ng, yl, np_, ml, 2)
    depth_back = depth_inverse(cells, kz)

    d = depth_lines(field.reshape(c, xl * yl, cells), depth.reshape(cells, 2 * kz).T, yl)
    d = swap(d.reshape(np_, cb, 2 * kz, xl * yl), "px")
    e = swap(rows_call(d, row, ng), "py")
    e = e.reshape(ng, cb, 2, kl, yl, kx)
    f = dot("hcskyj,shyqmt->qctmkj", e, column)
    f = swap(f, "px").reshape(c, 2, ml, kl, kx)
    mixed = mix_modes(jnp.transpose(f, (0, 1, 4, 2, 3)).astype(wide), spectral).astype(narrow)
    mixed = jnp.transpose(mixed, (0, 1, 3, 4, 2))
    b = swap(mixed.reshape(np_, cb, 2, ml, kl, kx), "px")
    b = dot("pcumkj,uhypmv->hcvkyj", b, column_back)
    b = swap(b.reshape(ng, cb, 2, kl, yl * kx), "py")
    b = swap(rows_back_call(b, row_back), "px")
    b = b.reshape(c, 2 * kz, xl * yl)
    return b, jnp.transpose(depth_back, (0, 2, 1)).reshape(2 * kz, cells)


def gelu(v):
    return 0.5 * v * (1.0 + jnp.tanh(math.sqrt(2.0 / math.pi) * (v + 0.044715 * v * v * v)))


def depth_kernel(yl, table, lines, out, held):
    points = lines.shape[1]
    for i in range(lines.shape[0]):
        cells = lines[i]
        if yl:
            held[...] = cells.astype(wide)
            cells = [held[pl.ds(y, points // yl, yl), :] for y in range(yl)]
            cells = jnp.concatenate(cells, 0).astype(narrow)
        out[i] = lax.dot_general(
            table[...], cells, (((1,), (1,)), ((), ())), preferred_element_type=wide
        ).astype(narrow)


def depth_lines(lines, table, yl=0):
    c, points, cells = lines.shape
    step = 4 if c % 4 == 0 else 1
    return pl.pallas_call(
        functools.partial(depth_kernel, yl),
        out_shape=jax.ShapeDtypeStruct((c, table.shape[0], points), narrow),
        grid=(c // step,),
        in_specs=[
            pl.BlockSpec(table.shape, lambda i: (0, 0)),
            pl.BlockSpec((step, points, cells), lambda i: (i, 0, 0)),
        ],
        out_specs=pl.BlockSpec((step, table.shape[0], points), lambda i: (i, 0, 0)),
        scratch_shapes=[pltpu.VMEM((points, cells), wide)],
        name="depth_lines",
    )(table, lines)


def spread(mixing, rows):
    c = mixing.shape[0]
    place = jnp.arange(c * rows)
    pick = (place[:, None] // rows == jnp.arange(c)[None, :]).astype(narrow)
    full = dot("on,np->op", pick, dot("nc,pc->np", mixing.T, pick), wide)
    return jnp.where(place[:, None] % rows == place[None, :] % rows, full, 0.0).astype(narrow)


def column_of(offsets, rows):
    return jnp.broadcast_to(offsets[:, None], (offsets.shape[0], rows)).reshape(-1, 1)


def back_along_depth(coefficients, table, sums, xl, yl):
    for o in range(sums.shape[0]):
        part = lax.dot_general(
            coefficients[o], table[...], (((0,), (0,)), ((), ())), preferred_element_type=wide
        )
        for y in range(yl):
            sums[o, pl.ds(y, xl, yl), :] = part[y * xl : (y + 1) * xl]


def upper_kernel(field, coefficients, table, mixing, offsets, pairs, upper, pooled, sums, half):
    c, xs, yl, cells = field.shape
    step = pl.program_id(0)

    @pl.when(step == 0)
    def _():
        back_along_depth(coefficients, table, sums, sums.shape[1] // yl, yl)

    for x in range(xs):
        lines = field[:, x].reshape(c * yl, cells)
        total = jnp.dot(mixing[...], lines, preferred_element_type=wide)
        total = total + sums[:, pl.ds(pl.multiple_of((step * xs + x) * yl, 8), yl), :].reshape(c * yl, cells) + offsets[...]
        value = gelu(total).astype(narrow)
        upper[:, x] = value.reshape(c, yl, cells)
        part = jnp.dot(value, pairs[...], preferred_element_type=wide)
        if x % 2 == 0:
            half[...] = part
        else:
            half[...] = half[...] + part
            rows = c * yl // 2
            mean = half[pl.ds(0, rows, 2), :] + half[pl.ds(1, rows, 2), :]
            mean = (mean * 0.125)[:, : cells // 2]
            pooled[:, x // 2] = mean.reshape(c, yl // 2, cells // 2).astype(narrow)


def upper_call(field, coefficients, table, mixing, offsets):
    c, xl, yl, cells = field.shape
    xs = 4
    place = jnp.arange(cells)
    pairs = (place[:, None] // 2 == place[None, :]).astype(narrow)
    whole = lambda value: pl.BlockSpec(value.shape, lambda i: (0,) * value.ndim)
    mixing = spread(mixing, yl)
    offsets = column_of(offsets, yl)
    return pl.pallas_call(
        upper_kernel,
        out_shape=(
            jax.ShapeDtypeStruct(field.shape, narrow),
            jax.ShapeDtypeStruct((c, xl // 2, yl // 2, cells // 2), narrow),
        ),
        grid=(xl // xs,),
        in_specs=[
            pl.BlockSpec((c, xs, yl, cells), lambda i: (0, i, 0, 0)),
            whole(coefficients),
            whole(table),
            whole(mixing),
            whole(offsets),
            whole(pairs),
        ],
        out_specs=(
            pl.BlockSpec((c, xs, yl, cells), lambda i: (0, i, 0, 0)),
            pl.BlockSpec((c, xs // 2, yl // 2, cells // 2), lambda i: (0, i, 0, 0)),
        ),
        scratch_shapes=[
            pltpu.VMEM((c, xl * yl, cells), wide),
            pltpu.VMEM((c * yl, cells), wide),
        ],
        compiler_params=pltpu.CompilerParams(vmem_limit_bytes=48 * 2**20),
        name="upper_call",
    )(field, coefficients, table, mixing, offsets, pairs)


def merge_kernel(upper, pooled, coefficients, table, mixing, offsets, twice, out, sums, lifted):
    c, xs, yl, cells = pooled.shape
    step = pl.program_id(0)

    @pl.when(step == 0)
    def _():
        back_along_depth(coefficients, table, sums, sums.shape[1] // yl, yl)

    for x in range(xs):
        lines = pooled[:, x].astype(wide).reshape(c * yl, cells).astype(narrow)
        total = jnp.dot(mixing[...], lines, preferred_element_type=wide)
        total = total + sums[:, pl.ds(pl.multiple_of((step * xs + x) * yl, 8), yl), :].reshape(c * yl, cells) + offsets[...]
        value = gelu(total).astype(narrow)
        wider = jnp.dot(value, twice[...], preferred_element_type=wide)
        lifted[pl.ds(0, c * yl, 2), :] = wider
        lifted[pl.ds(1, c * yl, 2), :] = wider
        for side in range(2):
            fine = upper[:, 2 * x + side].astype(wide).reshape(2 * c * yl, 2 * cells)
            out[:, 2 * x + side] = (fine + lifted[...]).astype(narrow).reshape(c, 2 * yl, 2 * cells)


def merge_call(upper, pooled, coefficients, table, mixing, offsets):
    c, xl, yl, cells = pooled.shape
    xs = 2
    twice = (jnp.arange(cells)[:, None] == jnp.arange(2 * cells)[None, :] // 2).astype(narrow)
    whole = lambda value: pl.BlockSpec(value.shape, lambda i: (0,) * value.ndim)
    mixing = spread(mixing, yl)
    offsets = column_of(offsets, yl)
    fine = pl.BlockSpec((c, 2 * xs, 2 * yl, 2 * cells), lambda i: (0, i, 0, 0))
    return pl.pallas_call(
        merge_kernel,
        out_shape=jax.ShapeDtypeStruct(upper.shape, narrow),
        grid=(xl // xs,),
        in_specs=[
            fine,
            pl.BlockSpec((c, xs, yl, cells), lambda i: (0, i, 0, 0)),
            whole(coefficients),
            whole(table),
            whole(mixing),
            whole(offsets),
            whole(twice),
        ],
        out_specs=fine,
        scratch_shapes=[
            pltpu.VMEM((c, xl * yl, cells), wide),
            pltpu.VMEM((2 * c * yl, 2 * cells), wide),
        ],
        compiler_params=pltpu.CompilerParams(vmem_limit_bytes=48 * 2**20),
        name="merge_call",
    )(upper, pooled, coefficients, table, mixing, offsets, twice)


def plain_layer(field, coefficients, table, mixing, offsets):
    c, xl, yl, cells = field.shape
    total = jnp.einsum("cnp,nz->cpz", coefficients, table, preferred_element_type=wide)
    total = total.reshape(field.shape)
    total = total + jnp.einsum("cxyz,co->oxyz", field, mixing, preferred_element_type=wide)
    return gelu(total + offsets[:, None, None, None]).astype(narrow)


def plain_pool(upper):
    c, xl, yl, cells = upper.shape
    blocks = upper.astype(wide).reshape(c, xl // 2, 2, yl // 2, 2, cells // 2, 2)
    return blocks.mean(axis=(2, 4, 6)).astype(narrow)


def plain_merge(upper, lower):
    c, xl, yl, cells = upper.shape
    blocks = upper.astype(wide).reshape(c, xl // 2, 2, yl // 2, 2, cells // 2, 2)
    merged = blocks + lower.astype(wide)[:, :, None, :, None, :, None]
    return merged.reshape(upper.shape).astype(narrow)


def on_device(field, spec_fine, mix_fine, bias_fine, spec_coarse, mix_coarse, bias_coarse):
    c, xl, yl, cells = field.shape
    tiled = yl % 16 == 0 and 128 % yl == 0 and (xl * yl) % 128 == 0 and xl % 4 == 0 and 128 % xl == 0
    find = tiled_coefficients if tiled else spectral_coefficients
    found, table = find(field, spec_fine)
    if tiled:
        upper, pooled = upper_call(field, found, table, mix_fine, bias_fine)
    else:
        upper = plain_layer(field, found, table, mix_fine, bias_fine)
        pooled = plain_pool(upper)
    found, table = find(pooled, spec_coarse)
    if tiled:
        return merge_call(upper, pooled, found, table, mix_coarse, bias_coarse)
    return plain_merge(upper, plain_layer(pooled, found, table, mix_coarse, bias_coarse))


def solution(mesh):
    return jax.shard_map(
        on_device,
        mesh=mesh,
        in_specs=(
            P(None, "px", "py", None),
            P(None, None, None, None, "px", "py"),
            P(),
            P(),
            P(None, None, None, None, "px", "py"),
            P(),
            P(),
        ),
        out_specs=P(None, "px", "py", None),
        check_vma=False,
    )
```

```python
import functools
import math

import jax
import jax.numpy as jnp
from jax import lax
from jax.experimental import pallas as pl
from jax.experimental.pallas import tpu as pltpu
from jax.sharding import PartitionSpec as P

narrow = jnp.bfloat16
wide = jnp.float32


def phases(cells, modes, offset):
    places = jnp.arange(cells, dtype=jnp.int32)
    frequency = jnp.arange(modes, dtype=jnp.int32) - offset
    windings = places[:, None] * frequency[None, :] % cells
    return windings.astype(wide) * (2.0 * math.pi / cells)


def turn_table(cells, modes, offset, sign):
    angle = phases(cells, modes, offset)
    cos = jnp.cos(angle).astype(narrow)
    sin = (sign * jnp.sin(angle)).astype(narrow)
    return jnp.stack([jnp.stack([cos, sin], -1), jnp.stack([-sin, cos], -1)])


def depth_forward(cells, modes):
    angle = phases(cells, modes, 0)
    return jnp.stack([jnp.cos(angle), -jnp.sin(angle)], 1).astype(narrow)


def depth_inverse(cells, modes):
    angle = phases(cells, modes, 0)
    factor = jnp.where(jnp.arange(modes) == 0, 1.0, 2.0).astype(wide) / float(cells * cells * cells)
    return jnp.stack([factor * jnp.cos(angle), -factor * jnp.sin(angle)]).astype(narrow)


def dot(form, left, right, kind=narrow):
    return jnp.einsum(form, left, right, preferred_element_type=wide).astype(kind)


def swap(value, axis):
    return lax.all_to_all(value, axis, split_axis=0, concat_axis=0)


def mix_modes(modes, spectral):
    mr = modes[:, 0][:, None]
    mi = modes[:, 1][:, None]
    wr = spectral[0].astype(wide)
    wi = spectral[1].astype(wide)
    real = (mr * wr - mi * wi).sum(0)
    imag = (mr * wi + mi * wr).sum(0)
    return jnp.stack([real, imag], 1)


def spectral_coefficients(field, spectral):
    np_, ng = lax.axis_size("px"), lax.axis_size("py")
    c, xl, yl, cells = field.shape
    _, _, _, kx, ml, kl = spectral.shape
    ky, kz = ml * np_, kl * ng
    cb = c // np_
    row = turn_table(cells, kx, kx // 2, -1.0).reshape(2, np_, xl, kx, 2)
    column = turn_table(cells, ky, ky // 2, -1.0).reshape(2, ng, yl, np_, ml, 2)
    depth = depth_forward(cells, kz)
    row_back = turn_table(cells, kx, kx // 2, 1.0).reshape(2, np_, xl, kx, 2)
    column_back = turn_table(cells, ky, ky // 2, 1.0).reshape(2, ng, yl, np_, ml, 2)
    depth_back = depth_inverse(cells, kz)

    d = depth_lines(field.reshape(c, xl * yl, cells), depth.reshape(cells, 2 * kz).T)
    d = swap(d.reshape(np_, cb, 2 * kz, xl * yl), "px").reshape(np_, cb, 2, ng, kl, xl, yl)
    e = dot("pcrgkxy,rpxjs->gcskjy", d, row)
    e = swap(e, "py")
    f = dot("hcskjy,shyqmt->qctjmk", e, column)
    f = swap(f, "px").reshape(c, 2, kx, ml, kl)
    mixed = mix_modes(f.astype(wide), spectral).astype(narrow)
    b = swap(mixed.reshape(np_, cb, 2, kx, ml, kl), "px")
    b = dot("pcujmk,uhypmv->hcvkjy", b, column_back)
    b = swap(b, "py")
    b = dot("gcvkjy,vpxjw->pcwgkxy", b, row_back)
    b = swap(b.reshape(np_, cb, 2 * kz, xl * yl), "px").reshape(c, 2 * kz, xl * yl)
    return b, jnp.transpose(depth_back, (0, 2, 1)).reshape(2 * kz, cells)


def line_tables(shape, split, cell_at, cells, offset, sign):
    near, far, quota = split
    iota = lambda axis: lax.broadcasted_iota(jnp.int32, shape, axis)
    row, column = iota(2), iota(3)
    cell, mode = (row % near, column % far) if cell_at == 0 else (column % far, row % near)
    blocks, part = (iota(0), iota(1)) if cell_at == 0 else (iota(1), iota(0))
    side = near if cell_at == 0 else far
    other = column // (quota * far)
    angle = ((blocks * side + cell) * (mode - offset) % cells).astype(wide) * (2.0 * math.pi / cells)
    sin = jnp.where(other == 1, sign, -sign) * jnp.sin(angle)
    value = jnp.where(part == other, jnp.cos(angle), sin)
    same = row // near == column // far % quota
    return jnp.where(same, value, 0.0).astype(narrow)


def rows_kernel(d, table, out):
    blocks, cs, both, _ = d.shape
    kz = both // 2
    groups, _, _, kl, _ = out.shape
    take, give = table.shape[2], table.shape[3] // 2
    for t in range(d.shape[3] // take):
        total = 0.0
        for p in range(blocks):
            for r in range(2):
                part = d[p, :, r * kz : (r + 1) * kz, t * take : (t + 1) * take]
                part = part.reshape(cs * kz, take)
                total = total + jnp.dot(part, table[p, r], preferred_element_type=wide)
        for s in range(2):
            for c in range(cs):
                for g in range(groups):
                    rows = total[c * kz + g * kl : c * kz + (g + 1) * kl, s * give : (s + 1) * give]
                    out[g, c, s, :, t * give : (t + 1) * give] = rows.astype(narrow)


def rows_call(d, table, groups):
    blocks, cb, both, points = d.shape
    take, give = table.shape[2], table.shape[3] // 2
    width = points // take * give
    kl = both // 2 // groups
    cs = 2 if cb % 2 == 0 else 1
    return pl.pallas_call(
        rows_kernel,
        out_shape=jax.ShapeDtypeStruct((groups, cb, 2, kl, width), narrow),
        grid=(cb // cs,),
        in_specs=[
            pl.BlockSpec((blocks, cs, both, points), lambda i: (0, i, 0, 0)),
            pl.BlockSpec(table.shape, lambda i: (0, 0, 0, 0)),
        ],
        out_specs=pl.BlockSpec((groups, cs, 2, kl, width), lambda i: (0, i, 0, 0, 0)),
        name="rows_call",
    )(d, table)


def rows_back_kernel(b, table, out, lines):
    groups, cs, _, kl, width = b.shape
    blocks = out.shape[0]
    kz = groups * kl
    take, give = table.shape[2], table.shape[3] // 2
    for v in range(2):
        for c in range(cs):
            for g in range(groups):
                at = c * kz + g * kl
                lines[v, at : at + kl, :] = b[g, c, v].astype(wide)
    for t in range(width // take):
        parts = [lines[v, :, t * take : (t + 1) * take].astype(narrow) for v in range(2)]
        for p in range(blocks):
            total = jnp.dot(parts[0], table[0, p], preferred_element_type=wide)
            total = total + jnp.dot(parts[1], table[1, p], preferred_element_type=wide)
            for w in range(2):
                rows = total[:, w * give : (w + 1) * give].reshape(cs, kz, give)
                out[p, :, w * kz : (w + 1) * kz, t * give : (t + 1) * give] = rows.astype(narrow)


def rows_back_call(b, table):
    groups, cb, _, kl, width = b.shape
    blocks = table.shape[1]
    take, give = table.shape[2], table.shape[3] // 2
    points = width // take * give
    kz = groups * kl
    cs = 2 if cb % 2 == 0 else 1
    return pl.pallas_call(
        rows_back_kernel,
        out_shape=jax.ShapeDtypeStruct((blocks, cb, 2 * kz, points), narrow),
        grid=(cb // cs,),
        in_specs=[
            pl.BlockSpec((groups, cs, 2, kl, width), lambda i: (0, i, 0, 0, 0)),
            pl.BlockSpec(table.shape, lambda i: (0, 0, 0, 0)),
        ],
        out_specs=pl.BlockSpec((blocks, cs, 2 * kz, points), lambda i: (0, i, 0, 0)),
        scratch_shapes=[pltpu.VMEM((2, cs * kz, width), wide)],
        name="rows_back_call",
    )(b, table)


def tiled_coefficients(field, spectral):
    np_, ng = lax.axis_size("px"), lax.axis_size("py")
    c, xl, yl, cells = field.shape
    _, _, _, kx, ml, kl = spectral.shape
    ky, kz = ml * np_, kl * ng
    cb = c // np_
    quota = min(yl, 128 // xl)
    row = line_tables(
        (np_, 2, quota * xl, 2 * quota * kx), (xl, kx, quota), 0, cells, kx // 2, -1.0
    )
    column = turn_table(cells, ky, ky // 2, -1.0).reshape(2, ng, yl, np_, ml, 2)
    depth = depth_forward(cells, kz)
    row_back = line_tables(
        (2, np_, quota * kx, 2 * quota * xl), (kx, xl, quota), 1, cells, kx // 2, 1.0
    )
    column_back = turn_table(cells, ky, ky // 2, 1.0).reshape(2, ng, yl, np_, ml, 2)
    depth_back = depth_inverse(cells, kz)

    d = depth_lines(field.reshape(c, xl * yl, cells), depth.reshape(cells, 2 * kz).T, yl)
    d = swap(d.reshape(np_, cb, 2 * kz, xl * yl), "px")
    e = swap(rows_call(d, row, ng), "py")
    e = e.reshape(ng, cb, 2, kl, yl, kx)
    f = dot("hcskyj,shyqmt->qctmkj", e, column)
    f = swap(f, "px").reshape(c, 2, ml, kl, kx)
    mixed = mix_modes(jnp.transpose(f, (0, 1, 4, 2, 3)).astype(wide), spectral).astype(narrow)
    mixed = jnp.transpose(mixed, (0, 1, 3, 4, 2))
    b = swap(mixed.reshape(np_, cb, 2, ml, kl, kx), "px")
    b = dot("pcumkj,uhypmv->hcvkyj", b, column_back)
    b = swap(b.reshape(ng, cb, 2, kl, yl * kx), "py")
    b = swap(rows_back_call(b, row_back), "px")
    b = b.reshape(c, 2 * kz, xl * yl)
    return b, jnp.transpose(depth_back, (0, 2, 1)).reshape(2 * kz, cells)


def gelu(v):
    return 0.5 * v * (1.0 + jnp.tanh(math.sqrt(2.0 / math.pi) * (v + 0.044715 * v * v * v)))


def depth_kernel(yl, table, lines, out, held):
    points = lines.shape[1]
    for i in range(lines.shape[0]):
        cells = lines[i]
        if yl:
            held[...] = cells.astype(wide)
            cells = [held[pl.ds(y, points // yl, yl), :] for y in range(yl)]
            cells = jnp.concatenate(cells, 0).astype(narrow)
        out[i] = lax.dot_general(
            table[...], cells, (((1,), (1,)), ((), ())), preferred_element_type=wide
        ).astype(narrow)


def depth_lines(lines, table, yl=0):
    c, points, cells = lines.shape
    step = 2 if c % 2 == 0 else 1
    return pl.pallas_call(
        functools.partial(depth_kernel, yl),
        out_shape=jax.ShapeDtypeStruct((c, table.shape[0], points), narrow),
        grid=(c // step,),
        in_specs=[
            pl.BlockSpec(table.shape, lambda i: (0, 0)),
            pl.BlockSpec((step, points, cells), lambda i: (i, 0, 0)),
        ],
        out_specs=pl.BlockSpec((step, table.shape[0], points), lambda i: (i, 0, 0)),
        scratch_shapes=[pltpu.VMEM((points, cells), wide)],
        name="depth_lines",
    )(table, lines)


def spread(mixing, rows):
    c = mixing.shape[0]
    place = jnp.arange(c * rows)
    pick = (place[:, None] // rows == jnp.arange(c)[None, :]).astype(narrow)
    full = dot("on,np->op", pick, dot("nc,pc->np", mixing.T, pick), wide)
    return jnp.where(place[:, None] % rows == place[None, :] % rows, full, 0.0).astype(narrow)


def column_of(offsets, rows):
    return jnp.broadcast_to(offsets[:, None], (offsets.shape[0], rows)).reshape(-1, 1)


def back_along_depth(coefficients, table, sums, xl, yl):
    for o in range(sums.shape[0]):
        part = lax.dot_general(
            coefficients[o], table[...], (((0,), (0,)), ((), ())), preferred_element_type=wide
        )
        for y in range(yl):
            sums[o, pl.ds(y, xl, yl), :] = part[y * xl : (y + 1) * xl]


def upper_kernel(field, coefficients, table, mixing, offsets, pairs, upper, pooled, sums, half):
    c, xs, yl, cells = field.shape
    step = pl.program_id(0)

    @pl.when(step == 0)
    def _():
        back_along_depth(coefficients, table, sums, sums.shape[1] // yl, yl)

    for x in range(xs):
        lines = field[:, x].reshape(c * yl, cells)
        total = jnp.dot(mixing[...], lines, preferred_element_type=wide)
        total = total + sums[:, pl.ds(pl.multiple_of((step * xs + x) * yl, 8), yl), :].reshape(c * yl, cells) + offsets[...]
        value = gelu(total).astype(narrow)
        upper[:, x] = value.reshape(c, yl, cells)
        part = jnp.dot(value, pairs[...], preferred_element_type=wide)
        if x % 2 == 0:
            half[...] = part
        else:
            half[...] = half[...] + part
            rows = c * yl // 2
            mean = half[pl.ds(0, rows, 2), :] + half[pl.ds(1, rows, 2), :]
            mean = (mean * 0.125)[:, : cells // 2]
            pooled[:, x // 2] = mean.reshape(c, yl // 2, cells // 2).astype(narrow)


def upper_call(field, coefficients, table, mixing, offsets):
    c, xl, yl, cells = field.shape
    xs = 4
    place = jnp.arange(cells)
    pairs = (place[:, None] // 2 == place[None, :]).astype(narrow)
    whole = lambda value: pl.BlockSpec(value.shape, lambda i: (0,) * value.ndim)
    mixing = spread(mixing, yl)
    offsets = column_of(offsets, yl)
    return pl.pallas_call(
        upper_kernel,
        out_shape=(
            jax.ShapeDtypeStruct(field.shape, narrow),
            jax.ShapeDtypeStruct((c, xl // 2, yl // 2, cells // 2), narrow),
        ),
        grid=(xl // xs,),
        in_specs=[
            pl.BlockSpec((c, xs, yl, cells), lambda i: (0, i, 0, 0)),
            whole(coefficients),
            whole(table),
            whole(mixing),
            whole(offsets),
            whole(pairs),
        ],
        out_specs=(
            pl.BlockSpec((c, xs, yl, cells), lambda i: (0, i, 0, 0)),
            pl.BlockSpec((c, xs // 2, yl // 2, cells // 2), lambda i: (0, i, 0, 0)),
        ),
        scratch_shapes=[
            pltpu.VMEM((c, xl * yl, cells), wide),
            pltpu.VMEM((c * yl, cells), wide),
        ],
        compiler_params=pltpu.CompilerParams(vmem_limit_bytes=48 * 2**20),
        name="upper_call",
    )(field, coefficients, table, mixing, offsets, pairs)


def merge_kernel(upper, pooled, coefficients, table, mixing, offsets, twice, out, sums, lifted):
    c, xs, yl, cells = pooled.shape
    step = pl.program_id(0)

    @pl.when(step == 0)
    def _():
        back_along_depth(coefficients, table, sums, sums.shape[1] // yl, yl)

    for x in range(xs):
        lines = pooled[:, x].astype(wide).reshape(c * yl, cells).astype(narrow)
        total = jnp.dot(mixing[...], lines, preferred_element_type=wide)
        total = total + sums[:, pl.ds(pl.multiple_of((step * xs + x) * yl, 8), yl), :].reshape(c * yl, cells) + offsets[...]
        value = gelu(total).astype(narrow)
        wider = jnp.dot(value, twice[...], preferred_element_type=wide)
        lifted[pl.ds(0, c * yl, 2), :] = wider
        lifted[pl.ds(1, c * yl, 2), :] = wider
        for side in range(2):
            fine = upper[:, 2 * x + side].astype(wide).reshape(2 * c * yl, 2 * cells)
            out[:, 2 * x + side] = (fine + lifted[...]).astype(narrow).reshape(c, 2 * yl, 2 * cells)


def merge_call(upper, pooled, coefficients, table, mixing, offsets):
    c, xl, yl, cells = pooled.shape
    xs = 2
    twice = (jnp.arange(cells)[:, None] == jnp.arange(2 * cells)[None, :] // 2).astype(narrow)
    whole = lambda value: pl.BlockSpec(value.shape, lambda i: (0,) * value.ndim)
    mixing = spread(mixing, yl)
    offsets = column_of(offsets, yl)
    fine = pl.BlockSpec((c, 2 * xs, 2 * yl, 2 * cells), lambda i: (0, i, 0, 0))
    return pl.pallas_call(
        merge_kernel,
        out_shape=jax.ShapeDtypeStruct(upper.shape, narrow),
        grid=(xl // xs,),
        in_specs=[
            fine,
            pl.BlockSpec((c, xs, yl, cells), lambda i: (0, i, 0, 0)),
            whole(coefficients),
            whole(table),
            whole(mixing),
            whole(offsets),
            whole(twice),
        ],
        out_specs=fine,
        scratch_shapes=[
            pltpu.VMEM((c, xl * yl, cells), wide),
            pltpu.VMEM((2 * c * yl, 2 * cells), wide),
        ],
        compiler_params=pltpu.CompilerParams(vmem_limit_bytes=48 * 2**20),
        name="merge_call",
    )(upper, pooled, coefficients, table, mixing, offsets, twice)


def plain_layer(field, coefficients, table, mixing, offsets):
    c, xl, yl, cells = field.shape
    total = jnp.einsum("cnp,nz->cpz", coefficients, table, preferred_element_type=wide)
    total = total.reshape(field.shape)
    total = total + jnp.einsum("cxyz,co->oxyz", field, mixing, preferred_element_type=wide)
    return gelu(total + offsets[:, None, None, None]).astype(narrow)


def plain_pool(upper):
    c, xl, yl, cells = upper.shape
    blocks = upper.astype(wide).reshape(c, xl // 2, 2, yl // 2, 2, cells // 2, 2)
    return blocks.mean(axis=(2, 4, 6)).astype(narrow)


def plain_merge(upper, lower):
    c, xl, yl, cells = upper.shape
    blocks = upper.astype(wide).reshape(c, xl // 2, 2, yl // 2, 2, cells // 2, 2)
    merged = blocks + lower.astype(wide)[:, :, None, :, None, :, None]
    return merged.reshape(upper.shape).astype(narrow)


def on_device(field, spec_fine, mix_fine, bias_fine, spec_coarse, mix_coarse, bias_coarse):
    c, xl, yl, cells = field.shape
    tiled = yl % 16 == 0 and 128 % yl == 0 and (xl * yl) % 128 == 0 and xl % 4 == 0 and 128 % xl == 0
    find = tiled_coefficients if tiled else spectral_coefficients
    found, table = find(field, spec_fine)
    if tiled:
        upper, pooled = upper_call(field, found, table, mix_fine, bias_fine)
    else:
        upper = plain_layer(field, found, table, mix_fine, bias_fine)
        pooled = plain_pool(upper)
    found, table = find(pooled, spec_coarse)
    if tiled:
        return merge_call(upper, pooled, found, table, mix_coarse, bias_coarse)
    return plain_merge(upper, plain_layer(pooled, found, table, mix_coarse, bias_coarse))


def solution(mesh):
    return jax.shard_map(
        on_device,
        mesh=mesh,
        in_specs=(
            P(None, "px", "py", None),
            P(None, None, None, None, "px", "py"),
            P(),
            P(),
            P(None, None, None, None, "px", "py"),
            P(),
            P(),
        ),
        out_specs=P(None, "px", "py", None),
        check_vma=False,
    )
```
